256 devices in a mesh: dp: 8 (over x, y_hi), row: 4 (over y_lo, core), col: 8 (over z).
Axes of the slice: x: 4, y: 4 (y_hi: 2, y_lo: 2; y = y_hi * 2 + y_lo), z: 8, core: 2. Of those that a mesh axis runs over, the one named last changes fastest.
Arguments:
- teacher_in: bfloat16 [8, 128, 256, 384], P('dp', 'row', 'col'), may hold values from -6 to 6
- student_in: bfloat16 [8, 128, 256, 384], P('dp', 'row', 'col'), may hold values from -6 to 6
- cotangent: bfloat16 [8, 128, 256, 384], P('dp', 'row', 'col'), may hold values from -6 to 6
- kernels: bfloat16 [2, 49, 384], replicated, may hold values from -0.875 to 0.875
- norm_gains: bfloat16 [2, 2, 384], replicated, may hold values from 0.25 to 1.75
- biases: bfloat16 [2, 3, 384], replicated, may hold values from -3 to 3
- weight_in: bfloat16 [2, 384, 1536], P(None, None, 'dp'), may hold values from -0.3125 to 0.3125
- bias_in: bfloat16 [2, 1536], P(None, 'dp'), may hold values from -3 to 3
- weight_out: bfloat16 [2, 1536, 384], P(None, 'dp'), may hold values from -0.15625 to 0.15625
Outputs:
- teacher_out: float32 [8, 128, 256, 384], P('dp', 'row', 'col')
- student_out: float32 [8, 128, 256, 384], P('dp', 'row', 'col')
- input_grad: float32 [8, 128, 256, 384], P('dp', 'row', 'col')
- grad_weight_in: float32 [384, 1536], P(None, 'dp')
- grad_bias_in: float32 [1536], P('dp')
- grad_weight_out: float32 [1536, 384], P('dp')
- grad_kernel: float32 [49, 384], replicated
- grad_gains: float32 [2, 384], replicated
- grad_biases: float32 [3, 384], replicated
The draws below stay inside these ranges and needn't reach their ends.
All inputs are finite; a program needn't handle non-finite values.
Results may differ from the reference program's by a relative error of at most 0.0057.
Values may be sent and summed in bfloat16 or wider, within the bound.
No kernel may reach another device: no remote copies, remote signals or barrier semaphores. Data moves between devices by JAX's collectives and lax.ppermute only.
A program may use at most 128 MiB of HBM per device.

```python
import jax
import jax.numpy as jnp
from jax import lax

C = 384
HID = 1536
KERNEL = 7
B = 8
H = 128
W = 256
TOKENS = 262144


def steps_of(key, extent, split, smallest, high):
    loudness, own = 1.0, jax.random.fold_in(key, 6)
    for axis_at, parts in split:
        draws = jnp.exp(jax.random.uniform(jax.random.fold_in(own, axis_at), (parts,), jnp.float32, smallest / len(split), high / len(split)))
        loudness = loudness * jnp.repeat(draws, extent[axis_at] // parts).reshape([-1 if axis == axis_at else 1 for axis in range(len(extent))])
    return loudness


def centred(own_key, extent, spread, reach, shards=(), held_as=jnp.bfloat16):
    level = steps_of(own_key, extent, shards, -0.22, 0.18) if shards else 1.0
    result = jax.random.normal(own_key, extent, jnp.float32) * spread * level
    return jnp.minimum(jnp.maximum(result, -reach), reach).astype(held_as)


def setup_inputs(seed: int = 0) -> dict:
    key_list = jax.random.split(jax.random.key(seed), 10)
    return {
        "teacher_in": centred(key_list[0], (B, H, W, C), 1.0, 6.0, ((0, 8), (1, 4), (2, 8))),
        "student_in": centred(key_list[1], (B, H, W, C), 1.0, 6.0, ((0, 8), (1, 4), (2, 8))),
        "cotangent": centred(key_list[2], (B, H, W, C), 1.0, 6.0, ((0, 8), (1, 4), (2, 8))),
        "kernels": centred(key_list[3], (2, KERNEL * KERNEL, C), (KERNEL * KERNEL) ** -0.5, 0.875),
        "norm_gains": jnp.clip(1.0 + 0.15 * jax.random.normal(key_list[4], (2, 2, C), jnp.float32), 0.25, 1.75).astype(jnp.bfloat16),
        "biases": centred(key_list[5], (2, 3, C), 0.5, 3.0),
        "weight_in": centred(key_list[6], (2, C, HID), C ** -0.5, 0.3125, ((2, 8),)),
        "bias_in": centred(key_list[7], (2, HID), 0.5, 3.0, ((1, 8),)),
        "weight_out": centred(key_list[8], (2, HID, C), HID ** -0.5, 0.15625, ((1, 8),)),
    }


EPSILON = 1e-06
ROOT_HALF = 0.7071067811865476
INV_ROOT_TWO_PI = 0.3989422804014327

def gelu_value(before):
    return before * 0.5 * (1.0 + lax.erf(before * ROOT_HALF))

def gelu_slope(before):
    return 0.5 * (1.0 + lax.erf(before * ROOT_HALF)) + before * INV_ROOT_TWO_PI * jnp.exp(-0.5 * before * before)

def depthwise(padded, kernel, height, breadth):
    running = jnp.zeros((padded.shape[0], height, breadth, padded.shape[3]), jnp.float32)
    for position in range(KERNEL * KERNEL):
        vertical = position // KERNEL
        lateral = position % KERNEL
        window = padded[:, vertical:vertical + height, lateral:lateral + breadth, :]
        running = running + window.astype(jnp.float32) * kernel[position].astype(jnp.float32)
    return running

def forward(padded, inputs, kernel, norm_gains, biases, weight_in, bias_in, weight_out):
    height, breadth, channels = (inputs.shape[1], inputs.shape[2], inputs.shape[3])
    convolved = depthwise(padded, kernel, height, breadth) + biases[0].astype(jnp.float32)
    centered = convolved - lax.optimization_barrier(jnp.mean(convolved, axis=-1, keepdims=True))
    inverse = lax.rsqrt(lax.optimization_barrier(jnp.mean(centered * centered, axis=-1, keepdims=True)) + EPSILON)
    scaled = centered * inverse
    normed = (scaled * norm_gains[0].astype(jnp.float32) + biases[1].astype(jnp.float32)).astype(jnp.bfloat16)
    normed = normed.reshape(-1, channels)
    before = jnp.dot(normed, weight_in, preferred_element_type=jnp.float32) + bias_in.astype(jnp.float32)
    hidden = gelu_value(before).astype(jnp.bfloat16)
    branch = jnp.dot(hidden, weight_out, preferred_element_type=jnp.float32) + biases[2].astype(jnp.float32)
    output = inputs.astype(jnp.float32) + norm_gains[1].astype(jnp.float32) * branch.reshape(inputs.shape)
    return (output, (scaled, inverse, normed, before, hidden, branch))

def backward(cotangent, padded, stored, kernel, norm_gains, weight_in, weight_out):
    scaled, inverse, normed, before, hidden, branch = stored
    height, breadth, channels = (cotangent.shape[1], cotangent.shape[2], cotangent.shape[3])
    flat_grad = cotangent.astype(jnp.float32).reshape(-1, channels)
    grad_gamma = lax.optimization_barrier(jnp.sum(flat_grad * branch, axis=0))
    branch_grad = (flat_grad * norm_gains[1].astype(jnp.float32)).astype(jnp.bfloat16)
    branch_grad = lax.optimization_barrier(branch_grad)
    grad_out_bias = lax.optimization_barrier(jnp.sum(branch_grad.astype(jnp.float32), axis=0))
    grad_weight_out = jnp.dot(hidden.T, branch_grad, preferred_element_type=jnp.float32)
    hidden_grad = jnp.dot(branch_grad, weight_out.T, preferred_element_type=jnp.float32)
    before_grad = (hidden_grad * gelu_slope(before)).astype(jnp.bfloat16)
    before_grad = lax.optimization_barrier(before_grad)
    grad_bias_in = lax.optimization_barrier(jnp.sum(before_grad.astype(jnp.float32), axis=0))
    grad_weight_in = jnp.dot(normed.T, before_grad, preferred_element_type=jnp.float32)
    normed_grad = jnp.dot(before_grad, weight_in.T, preferred_element_type=jnp.float32).reshape(scaled.shape)
    grad_norm_gain = lax.optimization_barrier(jnp.sum(normed_grad * scaled, axis=(0, 1, 2)))
    grad_norm_bias = lax.optimization_barrier(jnp.sum(normed_grad, axis=(0, 1, 2)))
    scaled_grad = normed_grad * norm_gains[0].astype(jnp.float32)
    conv_grad = inverse * (scaled_grad - lax.optimization_barrier(jnp.mean(scaled_grad, axis=-1, keepdims=True)) - scaled * lax.optimization_barrier(jnp.mean(scaled_grad * scaled, axis=-1, keepdims=True)))
    conv_grad = lax.optimization_barrier(conv_grad.astype(jnp.bfloat16))
    conv_wide = conv_grad.astype(jnp.float32)
    grad_conv_bias = lax.optimization_barrier(jnp.sum(conv_wide, axis=(0, 1, 2)))
    tap_sums = []
    for position in range(KERNEL * KERNEL):
        vertical = position // KERNEL
        lateral = position % KERNEL
        window = padded[:, vertical:vertical + height, lateral:lateral + breadth, :].astype(jnp.float32)
        tap_sums.append(lax.optimization_barrier(jnp.sum(window * conv_wide, axis=(0, 1, 2))))
    grad_kernel = jnp.stack(tap_sums)
    large_grads = (grad_weight_in, grad_bias_in, grad_weight_out)
    minor_grads = (grad_kernel, jnp.stack([grad_norm_gain, grad_gamma]), jnp.stack([grad_conv_bias, grad_norm_bias, grad_out_bias]))
    return (conv_grad, large_grads, minor_grads)

def input_gradient(cotangent, padded_grad, kernel):
    height, breadth = (cotangent.shape[1], cotangent.shape[2])
    flipped = depthwise(padded_grad, kernel[::-1], height, breadth)
    return cotangent.astype(jnp.float32) + flipped

def reference(teacher_in, student_in, cotangent, kernels, norm_gains, biases, weight_in, bias_in, weight_out):
    margin = KERNEL // 2
    widths = ((0, 0), (margin, margin), (margin, margin), (0, 0))

    def one_crop(crop_items):
        teacher_crop, student_crop, grad_crop = crop_items
        teacher_crop = teacher_crop[None]
        student_crop = student_crop[None]
        grad_crop = grad_crop[None]
        teacher_pad = jnp.pad(teacher_crop, widths)
        student_pad = jnp.pad(student_crop, widths)
        teacher_res, unused = forward(teacher_pad, teacher_crop, kernels[0], norm_gains[0], biases[0], weight_in[0], bias_in[0], weight_out[0])
        student_res, stored = forward(student_pad, student_crop, kernels[1], norm_gains[1], biases[1], weight_in[1], bias_in[1], weight_out[1])
        conv_grad, large_grads, minor_grads = backward(grad_crop, student_pad, stored, kernels[1], norm_gains[1], weight_in[1], weight_out[1])
        grad_pad = jnp.pad(conv_grad, widths)
        in_grad = input_gradient(grad_crop, grad_pad, kernels[1])
        return (teacher_res[0], student_res[0], in_grad[0]) + large_grads + minor_grads
    results = lax.map(one_crop, (teacher_in, student_in, cotangent))
    factor = TOKENS ** (-0.5)
    grads = tuple((lax.optimization_barrier(jnp.sum(item, axis=0)) * factor for item in results[3:]))
    return (results[0], results[1], results[2], grads[0], grads[1], grads[2], grads[3], grads[4], grads[5])
```

```python
import jax
import jax.numpy as jnp
from jax import lax
from jax.experimental import pallas as pl
from jax.experimental.pallas import tpu as pltpu
from jax.sharding import PartitionSpec as P

KERNEL = 7
EPSILON = 1e-06
ROOT_HALF = 0.7071067811865476
INV_ROOT_TWO_PI = 0.3989422804014327
H = 32
W = 32
C = 384
G = C // 128
HW = H * W
PAD_H = H + 6
PITCH = 48
LEFT = 8
F32 = jnp.float32
BF16 = jnp.bfloat16
AXES = ("dp", "row", "col")
DP, ROW, COL = 8, 4, 8
MINOR = 60


def flat(x, y, z, c):
    return ((x * 2 + y // 2) * ROW + (y % 2) * 2 + c) * COL + z


def send(value, target):
    pairs = []
    for x in range(4):
        for y in range(4):
            for z in range(COL):
                for c in range(2):
                    tx, ty, tz, tc = target(x, y, z, c)
                    pairs.append((flat(x, y, z, c), flat(tx % 4, ty, tz, tc)))
    return lax.ppermute(value, AXES, pairs)


def to_core(value):
    return send(value, lambda x, y, z, c: (x, y, z, 1 - c))


def shift(value, axis, up):
    peers = lax.axis_size(axis)
    pairs = [(i, i + 1) for i in range(peers - 1)]
    return lax.ppermute(value, axis, pairs if up else [(b, a) for a, b in pairs])


def halo(value):
    top = shift(value[:, H - 3 :], "row", True)
    bottom = shift(value[:, :3], "row", False)

    def columns(lo):
        return jnp.concatenate(
            [top[:, :, lo : lo + 3], value[:, :, lo : lo + 3], bottom[:, :, lo : lo + 3]], axis=1
        )

    left = shift(columns(W - 3), "col", True)
    right = shift(columns(0), "col", False)
    return top, bottom, left, right


def estimate(us):
    return pl.CostEstimate(flops=int(us * 1.0e9), bytes_accessed=4 << 20, transcendentals=0)


def lanes(g):
    return slice(g * 128, (g + 1) * 128)


def fill(pad, x_ref, top_ref, bottom_ref, left_ref, right_ref):
    def rows(i, _):
        for g in range(G):
            pad[g, i + 3, LEFT : LEFT + W, :] = x_ref[i, :, lanes(g)].astype(F32)
        return 0

    lax.fori_loop(0, H, rows, 0)
    for i in range(3):
        for g in range(G):
            pad[g, i, LEFT : LEFT + W, :] = top_ref[i, :, lanes(g)].astype(F32)
            pad[g, H + 3 + i, LEFT : LEFT + W, :] = bottom_ref[i, :, lanes(g)].astype(F32)

    def sides(i, _):
        for g in range(G):
            pad[g, i, LEFT - 3 : LEFT, :] = left_ref[i, :, lanes(g)].astype(F32)
            pad[g, i, LEFT + W : LEFT + W + 3, :] = right_ref[i, :, lanes(g)].astype(F32)
        return 0

    lax.fori_loop(0, PAD_H, sides, 0)


def convolve(pad, wide, flip, emit):
    def block(t, _):
        g, i0, j0 = t // 16, (t // 4 % 4) * 8, (t % 4) * 8
        sums = [None] * 8
        for e in range(KERNEL):
            taps = []
            for a in range(KERNEL):
                k = a * KERNEL + e
                taps.append(wide[g, KERNEL * KERNEL - 1 - k if flip else k])
            for r in range(8 + KERNEL - 1):
                x = pad[g, i0 + r, pl.ds(j0 + e + LEFT - 3, 8), :]
                for a in range(KERNEL):
                    o = r - a
                    if 0 <= o < 8:
                        term = x * taps[a]
                        sums[o] = term if sums[o] is None else sums[o] + term
        emit(g, i0, pl.multiple_of(j0, 8), sums)
        return 0

    lax.fori_loop(0, G * 16, block, 0)


def norm_kernel(
    x_ref, top_ref, bottom_ref, left_ref, right_ref, taps_ref, vec_ref,
    normed_ref, scaled_ref, inverse_ref, pad, conv,
):
    fill(pad, x_ref, top_ref, bottom_ref, left_ref, right_ref)

    def emit(g, i0, j0, sums):
        for o in range(8):
            conv[g, i0 + o, pl.ds(j0, 8), :] = sums[o]

    convolve(pad, taps_ref, False, emit)

    def rows(i, _):
        parts = [conv[g, i] + vec_ref[0:1, lanes(g)] for g in range(G)]
        mean = jnp.sum(parts[0] + parts[1] + parts[2], axis=1, keepdims=True) * (1.0 / C)
        parts = [p - mean for p in parts]
        square = parts[0] * parts[0] + parts[1] * parts[1] + parts[2] * parts[2]
        inverse = lax.rsqrt(jnp.sum(square, axis=1, keepdims=True) * (1.0 / C) + EPSILON)
        inverse_ref[i] = inverse
        for g in range(G):
            scaled = parts[g] * inverse
            scaled_ref[i, :, lanes(g)] = scaled
            normed = scaled * vec_ref[1:2, lanes(g)] + vec_ref[2:3, lanes(g)]
            normed_ref[i, :, lanes(g)] = normed.astype(BF16)
        return 0

    lax.fori_loop(0, H, rows, 0)


def norm_call(x, edges, taps, vec):
    return pl.pallas_call(
        norm_kernel,
        out_shape=(
            jax.ShapeDtypeStruct((H, W, C), BF16),
            jax.ShapeDtypeStruct((H, W, C), F32),
            jax.ShapeDtypeStruct((H, W, 1), F32),
        ),
        scratch_shapes=[
            pltpu.VMEM((G, PAD_H, PITCH, 128), F32),
            pltpu.VMEM((G, H, W, 128), F32),
        ],
        cost_estimate=estimate(9),
        name="conv_norm",
    )(x, *edges, taps, vec)


def input_kernel(
    x_ref, top_ref, bottom_ref, left_ref, right_ref, taps_ref, cot_ref, out_ref, pad
):
    fill(pad, x_ref, top_ref, bottom_ref, left_ref, right_ref)

    for g in range(G):

        def rows(i, _, g=g):
            out_ref[g, i] = cot_ref[i, :, lanes(g)].astype(F32)
            return 0

        lax.fori_loop(0, H, rows, 0)

    def emit(g, i0, j0, sums):
        for o in range(8):
            at = (g, i0 + o, pl.ds(j0, 8), slice(None))
            out_ref[at] = out_ref[at] + sums[o]

    convolve(pad, taps_ref, True, emit)


def input_kernel_final(*refs):
    *ins, out_ref, pad, total = refs
    input_kernel(*ins, total, pad)

    def rows(i, _):
        for g in range(G):
            out_ref[i, :, lanes(g)] = total[g, i]
        return 0

    lax.fori_loop(0, H, rows, 0)


def input_call(x, edges, taps, cot):
    return pl.pallas_call(
        input_kernel_final,
        out_shape=jax.ShapeDtypeStruct((H, W, C), F32),
        scratch_shapes=[
            pltpu.VMEM((G, PAD_H, PITCH, 128), F32),
            pltpu.VMEM((G, H, W, 128), F32),
        ],
        cost_estimate=estimate(8),
        name="input_grad",
    )(x, *edges, taps, cot)


def taps_kernel(
    x_ref, top_ref, bottom_ref, left_ref, right_ref, grad_ref, out_ref, pad, grad, sums
):
    fill(pad, x_ref, top_ref, bottom_ref, left_ref, right_ref)

    def rows(i, _):
        for g in range(G):
            grad[g, i] = grad_ref[i, :, lanes(g)].astype(F32)
        return 0

    lax.fori_loop(0, H, rows, 0)
    sums[...] = jnp.zeros_like(sums)

    def block(t, _):
        g, i0, j0 = t // 16, (t // 4 % 4) * 8, pl.multiple_of((t % 4) * 8, 8)
        cols = [grad[g, i0 + o, pl.ds(j0, 8), :] for o in range(8)]
        for e in range(KERNEL):
            part = [None] * KERNEL
            for r in range(8 + KERNEL - 1):
                x = pad[g, i0 + r, pl.ds(j0 + e + LEFT - 3, 8), :]
                for a in range(KERNEL):
                    o = r - a
                    if 0 <= o < 8:
                        term = x * cols[o]
                        part[a] = term if part[a] is None else part[a] + term
            for a in range(KERNEL):
                k = a * KERNEL + e
                sums[g, k] = sums[g, k] + part[a]
        total = cols[0]
        for o in range(1, 8):
            total = total + cols[o]
        sums[g, KERNEL * KERNEL] = sums[g, KERNEL * KERNEL] + total
        return 0

    lax.fori_loop(0, G * 16, block, 0)
    for g in range(G):
        out_ref[:, lanes(g)] = jnp.sum(sums[g], axis=1)


def taps_call(x, edges, grad):
    return pl.pallas_call(
        taps_kernel,
        out_shape=jax.ShapeDtypeStruct((56, C), F32),
        scratch_shapes=[
            pltpu.VMEM((G, PAD_H, PITCH, 128), F32),
            pltpu.VMEM((G, H, W, 128), F32),
            pltpu.VMEM((G, 56, 8, 128), F32),
        ],
        cost_estimate=estimate(8),
        name="tap_grad",
    )(x, *edges, grad)


def gelu_value(before):
    return before * 0.5 * (1.0 + lax.erf(before * ROOT_HALF))


def gelu_slope(before):
    return 0.5 * (1.0 + lax.erf(before * ROOT_HALF)) + before * INV_ROOT_TWO_PI * jnp.exp(
        -0.5 * before * before
    )


def mm(a, b, dims):
    return lax.dot_general(a, b, (dims, ((), ())), preferred_element_type=F32)


def mlp_forward(normed, inputs, gain, out_bias, w_in, b_in, w_out):
    before = mm(normed, w_in, ((1,), (0,))) + b_in
    hidden = gelu_value(before).astype(BF16)
    branch = mm(hidden, w_out, ((1,), (1,))) + out_bias
    out = inputs.reshape(HW, C).astype(F32) + gain * branch
    return out.reshape(1, H, W, C), before, hidden, branch


def mlp_backward(cot, normed, scaled, inverse, before, hidden, branch, gain, norm_gain, w_in, w_out):
    flat_cot = cot.reshape(HW, C).astype(F32)
    gamma = jnp.sum(flat_cot * branch, axis=0)
    branch_grad = lax.optimization_barrier((flat_cot * gain).astype(BF16))
    out_bias = jnp.sum(branch_grad.astype(F32), axis=0)
    w_out_grad = mm(branch_grad, hidden, ((0,), (0,)))
    hidden_grad = mm(branch_grad, w_out, ((1,), (0,)))
    before_grad = lax.optimization_barrier((hidden_grad * gelu_slope(before)).astype(BF16))
    b_in_grad = jnp.sum(before_grad.astype(F32), axis=0)
    w_in_grad = mm(normed, before_grad, ((0,), (0,)))
    normed_grad = mm(before_grad, w_in, ((1,), (1,)))
    norm_gain_grad = jnp.sum(normed_grad * scaled, axis=0)
    norm_bias_grad = jnp.sum(normed_grad, axis=0)
    scaled_grad = normed_grad * norm_gain
    conv_grad = inverse * (
        scaled_grad
        - jnp.mean(scaled_grad, axis=-1, keepdims=True)
        - scaled * jnp.mean(scaled_grad * scaled, axis=-1, keepdims=True)
    )
    small = [gamma, out_bias, norm_gain_grad, norm_bias_grad]
    return conv_grad.astype(BF16), w_in_grad, w_out_grad, b_in_grad, small


def gather_weights(w_in, b_in, w_out, core):
    mine = jnp.where(core == 0, w_in, w_out.T)
    mine = jnp.concatenate([mine, b_in[None], jnp.zeros((7, mine.shape[1]), BF16)], axis=0)
    pair = jnp.concatenate([mine, send(mine, lambda x, y, z, c: (x, y ^ 3, z, c))], axis=1)
    chunks = [pair]
    for k in (1, 2, 3):
        chunks.append(send(pair, lambda x, y, z, c, k=k: (x - k, y, z, c)))
    own = jnp.concatenate(chunks, axis=1)
    other = to_core(own)
    first, second = jnp.where(core == 0, own, other), jnp.where(core == 0, other, own)
    return first[:C], first[C : C + 1].astype(F32), second[:C]


def reduce_gradients(w_in_grad, w_out_grad, b_in_grad, minor, core):
    rows = C + 8
    bias = jnp.concatenate([b_in_grad[None], jnp.zeros((7, b_in_grad.shape[0]), F32)], axis=0)
    keep = jnp.concatenate([jnp.where(core == 0, w_in_grad, w_out_grad), bias], axis=0)
    away = jnp.concatenate([jnp.where(core == 0, w_out_grad, w_in_grad), bias], axis=0)
    pieces = [away[:, k * C : (k + 1) * C].astype(BF16) for k in range(4)]
    got = to_core(jnp.concatenate(pieces + [minor.astype(BF16)], axis=0)).astype(F32)
    minor = minor + got[4 * rows :]
    chunks = []
    for k in range(4):
        both = keep[:, k * C : (k + 1) * C] + got[k * rows : (k + 1) * rows]
        chunks.append(jnp.concatenate([both, minor], axis=0))
    total = chunks[0]
    for k in (1, 2, 3):
        piece = send(chunks[k].astype(BF16), lambda x, y, z, c, k=k: (x + k, y, z, c))
        total = total + piece.astype(F32)
    half = C // 2
    mine, theirs, minor = total[:rows, :half], total[:rows, half:], total[rows:]
    minor = minor.reshape(2 * MINOR, half)
    mine, theirs = jnp.concatenate([mine, minor], axis=0), jnp.concatenate([theirs, minor], axis=0)
    summed = mine
    for bits in (1, 2, 3):
        piece = (mine if bits == 1 else theirs).astype(BF16)
        summed = summed + send(piece, lambda x, y, z, c: (x, y ^ bits, z, c)).astype(F32)
    size = summed.shape[0] // COL
    parts = lax.all_to_all(summed.reshape(COL, size, half), "col", 0, 0, tiled=True)
    part = jnp.sum(parts, axis=0)
    parts = lax.all_to_all(
        jnp.broadcast_to(part[None], (COL, size, half)), "col", 0, 0, tiled=True
    )
    summed = parts.reshape(COL * size, half)
    own, minor = summed[:rows], summed[rows:].reshape(MINOR, C)
    other = to_core(own)
    first, second = jnp.where(core == 0, own, other), jnp.where(core == 0, other, own)
    return first[:C], first[C], second[:C].T, minor


def on_device(
    teacher_in, student_in, cotangent, kernels, norm_gains, biases, weight_in, bias_in, weight_out
):
    core = lax.axis_index("row") % 2
    inputs = (teacher_in, student_in)
    gains, offsets = norm_gains.astype(F32), biases.astype(F32)
    taps = kernels.astype(F32).reshape(2, KERNEL * KERNEL, G, 1, 128).transpose(0, 2, 1, 3, 4)
    taps = jnp.broadcast_to(taps, (2, G, KERNEL * KERNEL, 8, 128))
    edges = halo(jnp.concatenate([teacher_in, student_in], axis=0))
    weights = {}
    for s in (1, 0):
        weights[s] = gather_weights(weight_in[s], bias_in[s], weight_out[s], core)

    def norm(s):
        vec = jnp.concatenate(
            [offsets[s, 0][None], gains[s, 0][None], offsets[s, 1][None], jnp.zeros((5, C), F32)]
        )
        return norm_call(inputs[s][0], [e[s] for e in edges], taps[s], vec)

    def forward(s, normed):
        w_in, b_in, w_out = weights[s]
        return mlp_forward(
            normed.reshape(HW, C), inputs[s], gains[s, 1], offsets[s, 2], w_in, b_in, w_out
        )

    normed, scaled, inverse = norm(1)
    student_out, before, hidden, branch = forward(1, normed)
    conv_grad, w_in_grad, w_out_grad, b_in_grad, small = mlp_backward(
        cotangent, normed.reshape(HW, C), scaled.reshape(HW, C), inverse.reshape(HW, 1), before,
        hidden, branch, gains[1, 1], gains[1, 0], weights[1][0], weights[1][2],
    )
    gamma, out_bias, norm_gain_grad, norm_bias_grad = small
    conv_grad = conv_grad.reshape(1, H, W, C)
    grad_edges = halo(conv_grad)
    tap_sums = taps_call(student_in[0], [e[1] for e in edges], conv_grad[0])
    minor = jnp.concatenate(
        [
            tap_sums[: KERNEL * KERNEL],
            jnp.stack([norm_gain_grad, gamma]),
            jnp.stack([tap_sums[KERNEL * KERNEL], norm_bias_grad, out_bias]),
            jnp.zeros((MINOR - 54, C), F32),
        ]
    )
    tokens = HW * lax.axis_size("dp") * lax.axis_size("row") * lax.axis_size("col")
    factor = float(tokens) ** (-0.5)
    owned_in, owned_bias, owned_out, minor = reduce_gradients(
        w_in_grad, w_out_grad, b_in_grad, minor, core
    )
    in_grad = input_call(conv_grad[0], [e[0] for e in grad_edges], taps[1], cotangent[0])
    teacher_out, _, _, _ = forward(0, norm(0)[0])
    return (
        teacher_out,
        student_out,
        in_grad[None],
        owned_in * factor,
        owned_bias * factor,
        owned_out * factor,
        minor[:49] * factor,
        minor[49:51] * factor,
        minor[51:54] * factor,
    )


def solution(mesh):
    placed = (
        P("dp", "row", "col", None),
        P("dp", "row", "col", None),
        P("dp", "row", "col", None),
        P(),
        P(),
        P(),
        P(None, None, "dp"),
        P(None, "dp"),
        P(None, "dp", None),
    )
    step = jax.shard_map(
        on_device,
        mesh=mesh,
        in_specs=placed,
        out_specs=(
            P("dp", "row", "col", None),
            P("dp", "row", "col", None),
            P("dp", "row", "col", None),
            P(None, "dp"),
            P("dp"),
            P("dp", None),
            P(),
            P(),
            P(),
        ),
        check_vma=False,
    )

    def run(*args):
        with jax.sharding.use_abstract_mesh(mesh.abstract_mesh):
            return step(*args)

    return run
```

```python
import functools

import jax
import jax.numpy as jnp
from jax import lax
from jax.experimental import pallas as pl
from jax.experimental.pallas import tpu as pltpu
from jax.sharding import PartitionSpec as P

KERNEL = 7
EPSILON = 1e-06
ROOT_HALF = 0.7071067811865476
INV_ROOT_TWO_PI = 0.3989422804014327
H = 32
W = 32
C = 384
G = C // 128
HW = H * W
PAD_H = H + 6
PITCH = 48
LEFT = 8
F32 = jnp.float32
BF16 = jnp.bfloat16
AXES = ("dp", "row", "col")
DP, ROW, COL = 8, 4, 8
MINOR = 56


def flat(x, y, z, c):
    return ((x * 2 + y // 2) * ROW + (y % 2) * 2 + c) * COL + z


def send(value, target):
    pairs = []
    for x in range(4):
        for y in range(4):
            for z in range(COL):
                for c in range(2):
                    tx, ty, tz, tc = target(x, y, z, c)
                    pairs.append((flat(x, y, z, c), flat(tx % 4, ty, tz, tc)))
    return lax.ppermute(value, AXES, pairs)


def to_core(value):
    return send(value, lambda x, y, z, c: (x, y, z, 1 - c))


def shift(value, axis, up):
    peers = lax.axis_size(axis)
    pairs = [(i, i + 1) for i in range(peers - 1)]
    return lax.ppermute(value, axis, pairs if up else [(b, a) for a, b in pairs])


def halo(values):
    top = shift(jnp.concatenate([v[:, H - 3 :] for v in values]), "row", True)
    bottom = shift(jnp.concatenate([v[:, :3] for v in values]), "row", False)

    def columns(lo):
        middle = jnp.concatenate([v[:, :, lo : lo + 3] for v in values])
        return jnp.concatenate(
            [top[:, :, lo : lo + 3], middle, bottom[:, :, lo : lo + 3]], axis=1
        )

    left = shift(columns(W - 3), "col", True)
    right = shift(columns(0), "col", False)
    return top, bottom, left, right


def estimate(us):
    return pl.CostEstimate(flops=int(us * 1.0e9), bytes_accessed=4 << 20, transcendentals=0)


def params(mib):
    return pltpu.CompilerParams(vmem_limit_bytes=mib << 20)


def lanes(g):
    return slice(g * 128, (g + 1) * 128)


def fill(pad, x_ref, edges, s):
    top_ref, bottom_ref, left_ref, right_ref = (ref.at[s] for ref in edges)

    def rows(t, _):
        for u in range(4):
            i = t * 4 + u
            for g in range(G):
                pad[g, i + 3, LEFT : LEFT + W, :] = x_ref[i, :, lanes(g)].astype(F32)
        return 0

    lax.fori_loop(0, H // 4, rows, 0)
    for i in range(3):
        for g in range(G):
            pad[g, i, LEFT : LEFT + W, :] = top_ref[i, :, lanes(g)].astype(F32)
            pad[g, H + 3 + i, LEFT : LEFT + W, :] = bottom_ref[i, :, lanes(g)].astype(F32)

    def sides(t, _):
        for u in range(2):
            i = t * 2 + u
            for g in range(G):
                pad[g, i, LEFT - 3 : LEFT, :] = left_ref[i, :, lanes(g)].astype(F32)
                pad[g, i, LEFT + W : LEFT + W + 3, :] = right_ref[i, :, lanes(g)].astype(F32)
        return 0

    lax.fori_loop(0, PAD_H // 2, sides, 0)


def convolve(pad, wide, flip, emit):
    for g in range(G):

        def block(t, _, g=g):
            i0, j0 = (t // 4) * 8, (t % 4) * 8
            sums = [None] * 8
            for e in range(KERNEL):
                taps = []
                for a in range(KERNEL):
                    k = a * KERNEL + e
                    taps.append(wide[g, KERNEL * KERNEL - 1 - k if flip else k])
                for r in range(8 + KERNEL - 1):
                    x = pad[g, i0 + r, pl.ds(j0 + e + LEFT - 3, 8), :]
                    for a in range(KERNEL):
                        o = r - a
                        if 0 <= o < 8:
                            term = x * taps[a]
                            sums[o] = term if sums[o] is None else sums[o] + term
            emit(g, i0, pl.multiple_of(j0, 8), sums)
            return 0

        lax.fori_loop(0, 16, block, 0)


def norm_kernel(s, e, x_ref, *refs):
    edges, (taps_ref, vec_ref, normed_ref) = refs[:4], refs[4:7]
    scaled_ref, inverse_ref, pad, conv = refs[7:] if s else (None, None, *refs[7:])
    gain_row, offset_row, bias_row = 2 * s, 4 + 3 * s + 1, 4 + 3 * s
    fill(pad, x_ref, edges, e)

    def emit(g, i0, j0, sums):
        bias = jnp.broadcast_to(vec_ref[bias_row : bias_row + 1, lanes(g)], (8, 128))
        for o in range(8):
            conv[g, i0 + o, pl.ds(j0, 8), :] = sums[o] + bias

    convolve(pad, taps_ref.at[s], False, emit)

    def rows(t, _):
        at = pl.ds(t * 4, 4)
        parts = [conv[g, at] for g in range(G)]
        mean = jnp.sum(parts[0] + parts[1] + parts[2], axis=2, keepdims=True) * (1.0 / C)
        parts = [p - mean for p in parts]
        square = parts[0] * parts[0] + parts[1] * parts[1] + parts[2] * parts[2]
        inverse = lax.rsqrt(jnp.sum(square, axis=2, keepdims=True) * (1.0 / C) + EPSILON)
        if s:
            inverse_ref[at] = inverse
        for g in range(G):
            scaled = parts[g] * inverse
            if s:
                scaled_ref[at, :, lanes(g)] = scaled
            normed = scaled * vec_ref[gain_row : gain_row + 1, lanes(g)]
            normed = normed + vec_ref[offset_row : offset_row + 1, lanes(g)]
            normed_ref[at, :, lanes(g)] = normed.astype(BF16)
        return 0

    lax.fori_loop(0, H // 4, rows, 0)


def norm_call(s, e, x, edges, taps, vec):
    shapes = (
        jax.ShapeDtypeStruct((H, W, C), BF16),
        jax.ShapeDtypeStruct((H, W, C), F32),
        jax.ShapeDtypeStruct((H, W, 1), F32),
    )
    return pl.pallas_call(
        functools.partial(norm_kernel, s, e),
        out_shape=shapes if s else shapes[:1],
        scratch_shapes=[
            pltpu.VMEM((G, PAD_H, PITCH, 128), F32),
            pltpu.VMEM((G, H, W, 128), F32),
        ],
        cost_estimate=estimate(9),
        compiler_params=params(20),
        name="conv_norm",
    )(x, *edges, taps, vec)


def input_kernel(x_ref, *refs):
    edges, (taps_ref, cot_ref, out_ref, pad) = refs[:4], refs[4:]
    fill(pad, x_ref, edges, 0)

    def emit(g, i0, j0, sums):
        for o in range(8):
            at = (i0 + o, pl.ds(j0, 8), lanes(g))
            out_ref[at] = cot_ref[at].astype(F32) + sums[o]

    convolve(pad, taps_ref.at[1], True, emit)


def input_call(x, edges, taps, cot):
    return pl.pallas_call(
        input_kernel,
        out_shape=jax.ShapeDtypeStruct((H, W, C), F32),
        scratch_shapes=[pltpu.VMEM((G, PAD_H, PITCH, 128), F32)],
        cost_estimate=estimate(8),
        compiler_params=params(20),
        name="input_grad",
    )(x, *edges, taps, cot)


def taps_kernel(x_ref, *refs):
    edges, (grad_ref, small_ref, out_ref, pad, grad, sums) = refs[:4], refs[4:]
    fill(pad, x_ref, edges, 0)

    def rows(t, _):
        for u in range(4):
            for g in range(G):
                grad[g, t * 4 + u] = grad_ref[t * 4 + u, :, lanes(g)].astype(F32)
        return 0

    lax.fori_loop(0, H // 4, rows, 0)
    sums[...] = jnp.zeros_like(sums)

    def block(t, _):
        g, i0, j0 = t // 16, (t // 4 % 4) * 8, pl.multiple_of((t % 4) * 8, 8)
        cols = [grad[g, i0 + o, pl.ds(j0, 8), :] for o in range(8)]
        for e in range(KERNEL):
            part = [None] * KERNEL
            for r in range(8 + KERNEL - 1):
                x = pad[g, i0 + r, pl.ds(j0 + e + LEFT - 3, 8), :]
                for a in range(KERNEL):
                    o = r - a
                    if 0 <= o < 8:
                        term = x * cols[o]
                        part[a] = term if part[a] is None else part[a] + term
            for a in range(KERNEL):
                k = a * KERNEL + e
                sums[g, k] = sums[g, k] + part[a]
        total = cols[0]
        for o in range(1, 8):
            total = total + cols[o]
        sums[g, KERNEL * KERNEL] = sums[g, KERNEL * KERNEL] + total
        return 0

    lax.fori_loop(0, G * 16, block, 0)
    for g in range(G):
        total = jnp.sum(sums[g], axis=1)
        out_ref[0 : KERNEL * KERNEL, lanes(g)] = total[: KERNEL * KERNEL]
        out_ref[51:52, lanes(g)] = total[KERNEL * KERNEL : KERNEL * KERNEL + 1]
    out_ref[49:50, :] = small_ref[2:3, :]
    out_ref[50:51, :] = small_ref[0:1, :]
    out_ref[52:53, :] = small_ref[3:4, :]
    out_ref[53:54, :] = small_ref[1:2, :]
    out_ref[54:56, :] = jnp.zeros((2, C), F32)


def taps_call(x, edges, grad, small):
    return pl.pallas_call(
        taps_kernel,
        out_shape=jax.ShapeDtypeStruct((MINOR, C), F32),
        scratch_shapes=[
            pltpu.VMEM((G, PAD_H, PITCH, 128), F32),
            pltpu.VMEM((G, H, W, 128), F32),
            pltpu.VMEM((G, 56, 8, 128), F32),
        ],
        cost_estimate=estimate(8),
        compiler_params=params(20),
        name="tap_grad",
    )(x, *edges, grad, small)


HID = 1536
BIAS = C + 16
T = 256
STEP = C
ERF_P = 0.3275911
ERF_A = (0.254829592, -0.284496736, 1.421413741, -1.453152027, 1.061405429)


def mm(a, b, dims):
    return lax.dot_general(a, b, (dims, ((), ())), preferred_element_type=F32)


def gelu_parts(v):
    bell = jnp.exp(v * v * -0.5)
    t = 1.0 / (1.0 + (ERF_P * ROOT_HALF) * jnp.abs(v))
    tail = ERF_A[4]
    for c in ERF_A[3::-1]:
        tail = tail * t + c
    tail = tail * t * bell * 0.5
    return jnp.where(v >= 0.0, 1.0 - tail, tail), bell


def transfers(refs, weights, row, sems, core):
    out = []
    for n, ref in enumerate(refs):
        slot = core if n < 4 else 1 - core
        at = weights.at[slot, pl.ds((n % 4) * C, C), :]
        out.append(pltpu.make_async_copy(ref.at[pl.ds(0, C)], at, sems.at[n]))
        if n < 4:
            bias = ref.at[pl.ds(C, BIAS - C)]
            out.append(pltpu.make_async_copy(bias, row.at[n], sems.at[8 + n]))
    return out


def teacher_kernel(*refs):
    normed_ref, x_ref, vec_ref = refs[:3]
    chunks = refs[3:11]
    out_ref, weights, row, sems = refs[11:]
    copies = transfers(chunks, weights, row, sems, lax.axis_index("row") % 2)
    for copy in copies:
        copy.start()
    for copy in copies:
        copy.wait()

    def block(t, _):
        at = pl.ds(pl.multiple_of(t * T, T), T)
        normed = normed_ref[at, :]
        branch = None
        for n in range(HID // STEP):
            cols = slice(n * STEP, (n + 1) * STEP)
            before = mm(normed, weights[0, cols, :], ((1,), (1,)))
            before = before + row[n, 0:1, :].astype(F32)
            law, _ = gelu_parts(before)
            hidden = (before * law).astype(BF16)
            part = mm(hidden, weights[1, cols, :], ((1,), (0,)))
            branch = part if branch is None else branch + part
        branch = branch + vec_ref[6:7, :]
        out_ref[at, :] = x_ref[at, :].astype(F32) + vec_ref[1:2, :] * branch
        return 0

    lax.fori_loop(0, HW // T, block, 0)


def whole():
    return pl.BlockSpec(memory_space=pltpu.VMEM)


def teacher_call(normed, x, vec, chunks):
    return pl.pallas_call(
        teacher_kernel,
        in_specs=[whole()] * 3 + [pl.BlockSpec(memory_space=pl.ANY)] * 8,
        out_specs=whole(),
        out_shape=jax.ShapeDtypeStruct((HW, C), F32),
        scratch_shapes=[
            pltpu.VMEM((2, HID, C), BF16),
            pltpu.VMEM((4, BIAS - C, C), BF16),
            pltpu.SemaphoreType.DMA((12,)),
        ],
        cost_estimate=estimate(8),
        compiler_params=params(24),
        name="teacher_mlp",
    )(normed, x, vec, *chunks)


def fold(value):
    return jnp.sum(value.reshape(value.shape[0] // 8, 8, value.shape[1]), axis=0)


def student_kernel(*refs):
    normed_ref, scaled_ref, inverse_ref, x_ref, cot_ref, vec_ref = refs[:6]
    chunks = refs[6:14]
    out_ref, grad_ref, keep_ref, away_ref, small_ref = refs[14:19]
    weights, row, sems, hidden_s, slope_s, total, small, bias = refs[19:]
    core = lax.axis_index("row") % 2
    copies = transfers(chunks, weights, row, sems, core)
    for copy in copies:
        copy.start()
    total[...] = jnp.zeros_like(total)
    small[...] = jnp.zeros_like(small)
    bias[...] = jnp.zeros_like(bias)
    for copy in copies:
        copy.wait()

    def block(t, _):
        at = pl.ds(pl.multiple_of(t * T, T), T)
        normed = normed_ref[at, :]
        gain = vec_ref[3:4, :]
        branch = None
        for n in range(HID // STEP):
            cols = slice(n * STEP, (n + 1) * STEP)
            before = mm(normed, weights[0, cols, :], ((1,), (1,)))
            before = before + row[n, 0:1, :].astype(F32)
            law, bell = gelu_parts(before)
            hidden = (before * law).astype(BF16)
            hidden_s[:, cols] = hidden
            slope_s[:, cols] = law + before * (bell * INV_ROOT_TWO_PI)
            part = mm(hidden, weights[1, cols, :], ((1,), (0,)))
            branch = part if branch is None else branch + part
        branch = branch + vec_ref[9:10, :]
        out_ref[at, :] = x_ref[at, :].astype(F32) + gain * branch
        cot = cot_ref[at, :].astype(F32)
        small[0] += fold(cot * branch)
        branch_grad = (cot * gain).astype(BF16)
        small[1] += fold(branch_grad.astype(F32))
        normed_t, branch_t = normed.T, branch_grad.T
        normed_grad = None
        for n in range(HID // STEP):
            cols = slice(n * STEP, (n + 1) * STEP)
            hidden_grad = mm(branch_grad, weights[1, cols, :], ((1,), (1,)))
            before_grad = (hidden_grad * slope_s[:, cols]).astype(BF16)
            bias[:, cols] += fold(before_grad.astype(F32))
            total[core, :, cols] += mm(normed_t, before_grad, ((1,), (0,)))
            total[1 - core, :, cols] += mm(branch_t, hidden_s[:, cols], ((1,), (0,)))
            part = mm(before_grad, weights[0, cols, :], ((1,), (0,)))
            normed_grad = part if normed_grad is None else normed_grad + part
        scaled = scaled_ref[at, :]
        product = normed_grad * scaled
        small[2] += fold(product)
        small[3] += fold(normed_grad)
        norm_gain = vec_ref[2:3, :]
        scaled_grad = normed_grad * norm_gain
        mean = jnp.sum(scaled_grad, axis=1, keepdims=True) * (1.0 / C)
        along = jnp.sum(product * norm_gain, axis=1, keepdims=True) * (1.0 / C)
        conv_grad = inverse_ref[at, :] * (scaled_grad - mean - scaled * along)
        grad_ref[at, :] = conv_grad.astype(BF16)
        return 0

    lax.fori_loop(0, HW // T, block, 0)
    tail = jnp.broadcast_to(jnp.sum(bias[...], axis=0, keepdims=True), (BIAS - C, HID))
    for k in range(4):
        cols = slice(k * C, (k + 1) * C)
        keep_ref[k, :C, :] = total[0, :, cols]
        keep_ref[k, C:, :] = tail[:, cols]
        away_ref[k, :C, :] = total[1, :, cols].astype(BF16)
        away_ref[k, C:, :] = tail[:, cols].astype(BF16)
    for n in range(4):
        small_ref[n : n + 1, :] = jnp.sum(small[n], axis=0, keepdims=True)


def student_call(normed, scaled, inverse, x, cot, vec, chunks):
    return pl.pallas_call(
        student_kernel,
        in_specs=[whole()] * 6 + [pl.BlockSpec(memory_space=pl.ANY)] * 8,
        out_specs=[whole()] * 5,
        out_shape=(
            jax.ShapeDtypeStruct((HW, C), F32),
            jax.ShapeDtypeStruct((HW, C), BF16),
            jax.ShapeDtypeStruct((4, BIAS, C), F32),
            jax.ShapeDtypeStruct((4, BIAS, C), BF16),
            jax.ShapeDtypeStruct((4, C), F32),
        ),
        scratch_shapes=[
            pltpu.VMEM((2, HID, C), BF16),
            pltpu.VMEM((4, BIAS - C, C), BF16),
            pltpu.SemaphoreType.DMA((12,)),
            pltpu.VMEM((T, HID), BF16),
            pltpu.VMEM((T, HID), F32),
            pltpu.VMEM((2, C, HID), F32),
            pltpu.VMEM((4, 8, C), F32),
            pltpu.VMEM((8, HID), F32),
        ],
        cost_estimate=estimate(18),
        compiler_params=params(40),
        name="student_mlp",
    )(normed, scaled, inverse, x, cot, vec, *chunks)


def first_gather(w_in, b_in, w_out, core, *ahead):
    n = w_out.shape[0]
    row = jnp.pad(b_in[None], ((0, 15), (0, C - n)))
    mine = jnp.concatenate([jnp.where(core == 0, w_in.T, w_out), row], axis=0)
    if ahead:
        mine = after(mine, *ahead)
    got = send(mine, lambda x, y, z, c: (x, y ^ 3, z, c))
    row = jnp.concatenate([mine[n:, :n], got[n:, :n]], axis=1)
    return jnp.concatenate([mine[:n], got[:n], row], axis=0)


def along_x(pair):
    return [pair] + [send(pair, lambda x, y, z, c, k=k: (x - k, y, z, c)) for k in (1, 2, 3)]


def pack_kernel(keep_ref, got_ref, minor_ref, own_ref, *out_refs):
    own_ref[:BIAS, :] = keep_ref[0] + got_ref[0].astype(F32)
    own_ref[BIAS:, :] = minor_ref[...]
    for k in (1, 2, 3):
        out_refs[k - 1][:BIAS, :] = (keep_ref[k] + got_ref[k].astype(F32)).astype(BF16)
        out_refs[k - 1][BIAS:, :] = minor_ref[...].astype(BF16)


def pack_call(keep, got, minor):
    wire = jax.ShapeDtypeStruct((BIAS + MINOR, C), BF16)
    return pl.pallas_call(
        pack_kernel,
        out_shape=(jax.ShapeDtypeStruct((BIAS + MINOR, C), F32), wire, wire, wire),
        cost_estimate=estimate(2),
        compiler_params=params(16),
        name="pack",
    )(keep, got, minor)


def split_kernel(own_ref, one_ref, two_ref, three_ref, mine_ref, near_ref, far_ref, there):
    half = C // 2
    total = own_ref[...] + one_ref[...].astype(F32)
    total = total + two_ref[...].astype(F32) + three_ref[...].astype(F32)
    left, right = total[:, :half], total[:, half:]
    mine_ref[: BIAS + MINOR, :] = left
    mine_ref[BIAS + MINOR :, :] = right[BIAS:]
    there[:BIAS, :] = right[:BIAS]
    there[BIAS : BIAS + MINOR, :] = left[BIAS:]
    there[BIAS + MINOR :, :] = right[BIAS:]
    near_ref[...] = mine_ref[...].astype(BF16)
    far_ref[...] = there[...].astype(BF16)


def split_call(own, one, two, three):
    shape = (BIAS + 2 * MINOR, C // 2)
    return pl.pallas_call(
        split_kernel,
        out_shape=(
            jax.ShapeDtypeStruct(shape, F32),
            jax.ShapeDtypeStruct(shape, BF16),
            jax.ShapeDtypeStruct(shape, BF16),
        ),
        scratch_shapes=[pltpu.VMEM(shape, F32)],
        cost_estimate=estimate(2),
        compiler_params=params(16),
        name="split",
    )(own, one, two, three)


def finish_kernel(factor, own_ref, other_ref, in_ref, bias_ref, out_ref, tap_ref, gain_ref, off_ref):
    half = C // 2
    core = lax.axis_index("row") % 2

    def put(first_ref, second_ref):
        in_ref[...] = (first_ref[:C, :] * factor).T
        bias_ref[...] = first_ref[C : C + 1, :] * factor
        out_ref[...] = (second_ref[:C, :] * factor).T

    @pl.when(core == 0)
    def _():
        put(own_ref, other_ref)

    @pl.when(core == 1)
    def _():
        put(other_ref, own_ref)

    minor = (own_ref[BIAS:, :] + other_ref[BIAS:, :]) * factor
    minor = jnp.concatenate([minor[:MINOR], minor[MINOR:]], axis=1)
    tap_ref[...] = minor[:49]
    gain_ref[...] = minor[49:51]
    off_ref[...] = minor[51:54]


def finish_call(factor, own, other):
    half = C // 2
    shapes = ((half, C), (1, half), (half, C), (49, C), (2, C), (3, C))
    return pl.pallas_call(
        functools.partial(finish_kernel, factor),
        out_shape=tuple(jax.ShapeDtypeStruct(shape, F32) for shape in shapes),
        cost_estimate=estimate(2),
        compiler_params=params(16),
        name="finish",
    )(own, other)


def after(value, *others):
    return lax.optimization_barrier((value, *others))[0]


def on_device(
    teacher_in, student_in, cotangent, kernels, norm_gains, biases, weight_in, bias_in, weight_out
):
    core = lax.axis_index("row") % 2
    taps = kernels.astype(F32).reshape(2, KERNEL * KERNEL, G, 1, 128).transpose(0, 2, 1, 3, 4)
    taps = jnp.broadcast_to(taps, (2, G, KERNEL * KERNEL, 8, 128))
    vec = jnp.concatenate([norm_gains.reshape(4, C), biases.reshape(6, C)]).astype(F32)
    student, teacher, cot = student_in[0], teacher_in[0], cotangent[0]

    edges = halo((student_in, teacher_in))
    pair = first_gather(weight_in[1], bias_in[1], weight_out[1], core)
    own = along_x(pair)
    theirs = first_gather(weight_in[0], bias_in[0], weight_out[0], core, pair)
    normed, scaled, inverse = norm_call(1, 0, student, edges, taps, vec)
    own = lax.optimization_barrier((*own, normed))[:4]
    others = along_x(after(theirs, normed))
    chunks = [*own, *(to_core(chunk) for chunk in own)]
    student_out, conv_grad, keep, away, small = student_call(
        normed.reshape(HW, C), scaled.reshape(HW, C), inverse.reshape(HW, 1),
        student.reshape(HW, C), cot.reshape(HW, C), vec, chunks,
    )
    conv_grad = conv_grad.reshape(H, W, C)
    got = to_core(away)
    grad_edges = halo((conv_grad[None],))
    small, *others = lax.optimization_barrier((small, *others))
    minor = taps_call(student, edges, conv_grad, small)

    total, *wires = pack_call(keep, got, minor)
    pieces = [
        send(wires[k - 1], lambda x, y, z, c, k=k: (x + k, y, z, c)) for k in (1, 2, 3)
    ]
    in_grad = input_call(after(conv_grad, *wires), grad_edges, taps, cot)
    in_grad, *pieces = lax.optimization_barrier((in_grad, *pieces))
    summed, near, far = split_call(total, *pieces)
    for bits in (1, 2, 3):
        piece = near if bits == 1 else far
        summed = summed + send(piece, lambda x, y, z, c: (x, y ^ bits, z, c)).astype(F32)
    size, half = summed.shape[0] // COL, C // 2
    parts = lax.all_to_all(summed.reshape(COL, size, half), "col", 0, 0, tiled=True)
    (normed,) = norm_call(0, 1, after(teacher, summed), edges, taps, vec)
    others = [*others, *(to_core(chunk) for chunk in others)]
    parts, normed = lax.optimization_barrier((parts, normed))
    part = jnp.sum(parts, axis=0)
    parts = lax.all_to_all(
        jnp.broadcast_to(part[None], (COL, size, half)), "col", 0, 0, tiled=True
    )
    teacher_out = teacher_call(normed.reshape(HW, C), teacher.reshape(HW, C), vec, others)
    parts, teacher_out = lax.optimization_barrier((parts, teacher_out))
    mine = parts.reshape(COL * size, half)
    tokens = HW * lax.axis_size("dp") * lax.axis_size("row") * lax.axis_size("col")
    owned_in, owned_bias, owned_out, *minors = finish_call(
        float(tokens) ** (-0.5), mine, to_core(mine)
    )
    return (
        teacher_out.reshape(1, H, W, C),
        student_out.reshape(1, H, W, C),
        in_grad[None],
        owned_in.T,
        owned_bias.reshape(C // 2),
        owned_out,
        *minors,
    )


def solution(mesh):
    placed = (
        P("dp", "row", "col", None),
        P("dp", "row", "col", None),
        P("dp", "row", "col", None),
        P(),
        P(),
        P(),
        P(None, None, "dp"),
        P(None, "dp"),
        P(None, "dp", None),
    )
    step = jax.shard_map(
        on_device,
        mesh=mesh,
        in_specs=placed,
        out_specs=(
            P("dp", "row", "col", None),
            P("dp", "row", "col", None),
            P("dp", "row", "col", None),
            P(None, "dp"),
            P("dp"),
            P("dp", None),
            P(),
            P(),
            P(),
        ),
        check_vma=False,
    )

    def run(*args):
        with jax.sharding.use_abstract_mesh(mesh.abstract_mesh):
            return step(*args)

    return run
```
